32 devices in a mesh: rows: 8 (over y, x, core), cols: 4 (over z).
Axes of the slice: x: 2, y: 2, z: 4, core: 2. Of those that a mesh axis runs over, the one named last changes fastest.
Arguments:
- latent: float32 [1, 512, 512, 128], P(None, 'rows', 'cols'), may hold values from -6 to 6
- w_small: float32 [512, 128], replicated, may hold values from -0.25 to 0.25
- w_large: float32 [2048, 128], replicated, may hold values from -0.125 to 0.125
- gain_embed: float32 [256], replicated, may hold values from 0.1 to 1.9
- gain_attn: float32 [256], replicated, may hold values from 0.1 to 1.9
- w_qkv: float32 [256, 768], replicated, may hold values from -8 to 8
- pos_bias: float32 [8, 16, 16], replicated, may hold values from -4 to 4
- w_proj: float32 [256, 256], replicated, may hold values from -0.375 to 0.375
- gain_mlp: float32 [256], replicated, may hold values from 0.1 to 1.9
- w_up: float32 [256, 1024], replicated, may hold values from -0.375 to 0.375
- w_down: float32 [1024, 256], replicated, may hold values from -0.1875 to 0.1875
Outputs:
- result: float32 [1, 256, 256, 256], P(None, 'rows', 'cols')
The draws below stay inside these ranges and needn't reach their ends.
All inputs are finite; a program needn't handle non-finite values.
Results may differ from the reference program's by a relative error of at most 0.0003.
Values sent between devices are 32-bit elements; how exact they have to be, the bound alone decides.
A program may use at most 192 MiB of HBM per device.

```python
import jax
import jax.numpy as jnp
from jax import lax

BATCH = 1
INTV = 64
CIN = 128
C = 256
HEADS = 8
FF = 1024
CE = 128
HD = 32
H = 256
W = 256
GR = 4
GT = 16


def draw_w_qkv(key, part):
    base = jax.random.normal(key, (C, 3 * C), jnp.float32) / jnp.sqrt(jnp.float32(C))
    return jnp.clip(base, -8.0, 8.0)


def block_scale(rng, shape, pieces, smallest, high):
    level = 1.0
    for position, shards_of in pieces:
        draws = jax.random.uniform(jax.random.fold_in(jax.random.fold_in(rng, 6), position), (shards_of,), jnp.float32, smallest / len(pieces), high / len(pieces))
        level = level * jnp.repeat(jnp.exp(draws), shape[position] // shards_of).reshape((-1,) + (1,) * (len(shape) - 1 - position))
    return level


def scatter_about(own_key, extent, scale, reach, split=(), kind=jnp.bfloat16):
    entries = scale * jax.random.normal(own_key, extent, jnp.float32)
    if split:
        entries = entries * block_scale(own_key, extent, split, -0.22, 0.18)
    return jnp.clip(entries, -reach, reach).astype(kind)


def setup_inputs(seed: int = 0) -> dict:
    streams_of = jax.random.split(jax.random.key(seed), 12)
    return {
        "latent": scatter_about(streams_of[0], (BATCH, 2 * H, 2 * W, CIN), 1.0, 6.0, ((1, 8), (2, 4)), jnp.float32),
        "w_small": scatter_about(streams_of[1], (4 * CIN, CE), (4 * CIN) ** -0.5, 0.25, (), jnp.float32),
        "w_large": scatter_about(streams_of[2], (16 * CIN, CE), (16 * CIN) ** -0.5, 0.125, (), jnp.float32),
        "gain_embed": jnp.clip(1.0 + 0.18 * jax.random.normal(streams_of[3], (C,), jnp.float32), 0.1, 1.9),
        "gain_attn": jnp.clip(1.0 + 0.18 * jax.random.normal(streams_of[4], (C,), jnp.float32), 0.1, 1.9),
        "w_qkv": draw_w_qkv(jax.random.fold_in(streams_of[11], 71), 0),
        "pos_bias": scatter_about(streams_of[6], (HEADS, GT, GT), 1.0, 4.0, (), jnp.float32),
        "w_proj": scatter_about(streams_of[7], (C, C), C ** -0.5, 0.375, (), jnp.float32),
        "gain_mlp": jnp.clip(1.0 + 0.18 * jax.random.normal(streams_of[8], (C,), jnp.float32), 0.1, 1.9),
        "w_up": scatter_about(streams_of[9], (C, FF), C ** -0.5, 0.375, (), jnp.float32),
        "w_down": scatter_about(streams_of[10], (FF, C), FF ** -0.5, 0.1875, (), jnp.float32),
    }


def matmul(left, right):
    return jnp.dot(left, right, precision=lax.Precision.HIGHEST, preferred_element_type=jnp.float32)

def layer_norm(values, gain):
    center = values - lax.optimization_barrier(jnp.mean(values, axis=-1, keepdims=True))
    spread = lax.optimization_barrier(jnp.mean(center * center, axis=-1, keepdims=True))
    return center * lax.rsqrt(spread + 1e-05) * gain

def reference(latent, w_small, w_large, gain_embed, gain_attn, w_qkv, pos_bias, w_proj, gain_mlp, w_up, w_down):
    patches = latent.reshape(BATCH, H, 2, W, 2, CIN).transpose(0, 1, 3, 2, 4, 5).reshape(-1, 4 * CIN)
    small = matmul(patches, w_small)
    padded = jnp.pad(latent, ((0, 0), (1, 1), (1, 1), (0, 0)))
    large = jnp.zeros((BATCH * H * W, CE), jnp.float32)
    for row_shift in range(4):
        for col_shift in range(4):
            piece = padded[:, row_shift:row_shift + 2 * H:2, col_shift:col_shift + 2 * W:2, :].reshape(-1, CIN)
            first = (row_shift * 4 + col_shift) * CIN
            large = large + matmul(piece, w_large[first:first + CIN])
    embedded = layer_norm(jnp.concatenate([small, large], axis=-1), gain_embed)
    grouped = embedded.reshape(BATCH, GR, INTV, W // INTV, INTV, C).transpose(0, 2, 4, 1, 3, 5)
    grouped = grouped.reshape(BATCH * INTV, INTV, GT, C)
    scale = 1.0 / jnp.sqrt(jnp.float32(HD))

    def block(tokens):
        normed = layer_norm(tokens, gain_attn)
        qkv = matmul(normed.reshape(-1, C), w_qkv).reshape(INTV, GT, 3, HEADS, HD)
        scores = jnp.einsum('gqhd,gkhd->ghqk', qkv[:, :, 0], qkv[:, :, 1], precision=lax.Precision.HIGHEST) * scale + pos_bias[None]
        top = lax.optimization_barrier(jnp.max(scores, axis=-1, keepdims=True))
        expd = jnp.exp(scores - top)
        probs = expd / lax.optimization_barrier(jnp.sum(expd, axis=-1, keepdims=True))
        mixed = jnp.einsum('ghqk,gkhd->gqhd', probs, qkv[:, :, 2], precision=lax.Precision.HIGHEST).reshape(-1, C)
        after = tokens.reshape(-1, C) + matmul(mixed, w_proj)
        hidden = jax.nn.gelu(matmul(layer_norm(after, gain_mlp), w_up), approximate=False)
        return (after + matmul(hidden, w_down)).reshape(INTV, GT, C)
    output = lax.map(block, grouped)
    output = output.reshape(BATCH, INTV, INTV, GR, W // INTV, C).transpose(0, 3, 1, 4, 2, 5)
    return output.reshape(BATCH, H, W, C)
```

```python
import functools

import jax
import jax.numpy as jnp
from jax import lax
from jax.experimental import pallas as pl
from jax.experimental.pallas import tpu as pltpu
from jax.sharding import PartitionSpec as P

HEADS = 8
STAGES = 4
MESH = pl.DeviceIdType.MESH
F32 = jnp.float32
BF16 = jnp.bfloat16


def split(values):
    high = values.astype(BF16)
    return high, (values - high.astype(F32)).astype(BF16)


def dot(left, right, dims=((1,), (0,))):
    return lax.dot_general(left, right, (dims, ((), ())), preferred_element_type=F32)


def dot3(left, right, dims=((1,), (0,))):
    left_hi, left_lo = left
    right_hi, right_lo = right
    return (
        dot(left_hi, right_lo, dims) + dot(left_lo, right_hi, dims) + dot(left_hi, right_hi, dims)
    )


def layer_norm(values, gain):
    center = values - jnp.mean(values, axis=-1, keepdims=True)
    spread = jnp.mean(center * center, axis=-1, keepdims=True)
    return center * lax.rsqrt(spread + 1e-05) * gain


def gelu(values):
    return 0.5 * values * (1.0 + lax.erf(values * 0.7071067811865476))


def block_kernel(
    sizes,
    lat, w_small, w_large, gain_embed, gain_attn, w_qkv, pos_bias, w_proj, gain_mlp, w_up, w_down,
    out,
    eo_hi, eo_lo, oe_hi, oe_lo, wc, we, wo, wq, wp, wu, wd, bias,
    emb, recv, done, row_halo, col_halo, corner_halo, col_edge,
    halo_send, halo_recv, go_send, go_recv, back_send, back_recv,
):
    row_count, col_count, members, phases = sizes
    rows, cols, chan = lat.shape
    tile_rows, tile_cols = rows // 2, cols // 2
    feat = gain_embed.shape[1]
    half = feat // 2
    stage_rows = tile_rows // STAGES
    stage_tokens = stage_rows * tile_cols
    share = stage_tokens // members
    groups = max(8, min(share, 256 // members))
    tokens = members * groups
    head = feat // HEADS

    r = lax.axis_index("rows")
    c = lax.axis_index("cols")
    core = lax.rem(r, phases)
    me = (r // phases) * col_count + c

    def place(member):
        return (member // col_count) * phases + core, lax.rem(member, col_count)

    def other(step):
        return lax.rem(me + step, members)

    barrier = pltpu.get_barrier_semaphore()

    def greet(step, carry):
        pl.semaphore_signal(barrier, inc=1, device_id=place(other(step)), device_id_type=MESH)
        return carry

    lax.fori_loop(1, members, greet, 0)
    up, down = r > 0, r < row_count - 1
    west, east = c > 0, c < col_count - 1
    for row_ok, dr in ((up, -1), (down, 1)):
        for col_ok, dc in ((True, 0), (west, -1), (east, 1)):
            ok = row_ok if col_ok is True else jnp.logical_and(row_ok, col_ok)

            @pl.when(ok)
            def _(dr=dr, dc=dc):
                pl.semaphore_signal(barrier, inc=1, device_id=(r + dr, c + dc), device_id_type=MESH)

    col_edge[0] = lat[:, 0, :]
    col_edge[1] = lat[:, cols - 1, :]
    number = lambda flag: jnp.where(flag, 1, 0)
    vertical = number(up) + number(down)
    horizontal = 1 + number(west) + number(east)
    pl.semaphore_wait(barrier, members - 1 + vertical * horizontal)

    both = jnp.logical_and
    plan = [
        (up, down, (r - 1, c), lat.at[0], row_halo.at[1]),
        (down, up, (r + 1, c), lat.at[rows - 1], row_halo.at[0]),
        (west, east, (r, c - 1), col_edge.at[0], col_halo.at[1, pl.ds(8, rows)]),
        (east, west, (r, c + 1), col_edge.at[1], col_halo.at[0, pl.ds(8, rows)]),
        (both(up, west), both(down, east), (r - 1, c - 1), lat.at[0, pl.ds(0, 8)], corner_halo.at[3]),
        (both(up, east), both(down, west), (r - 1, c + 1), lat.at[0, pl.ds(cols - 8, 8)], corner_halo.at[2]),
        (both(down, west), both(up, east), (r + 1, c - 1), lat.at[rows - 1, pl.ds(0, 8)], corner_halo.at[1]),
        (both(down, east), both(up, west), (r + 1, c + 1), lat.at[rows - 1, pl.ds(cols - 8, 8)], corner_halo.at[0]),
    ]

    def halo_copy(index):
        _, _, target, source, destination = plan[index]
        return pltpu.make_async_remote_copy(
            src_ref=source, dst_ref=destination, send_sem=halo_send.at[index],
            recv_sem=halo_recv.at[index], device_id=target, device_id_type=MESH,
        )

    for index in range(8):
        @pl.when(plan[index][0])
        def _(index=index):
            halo_copy(index).start()

    def keep(ref, index, values):
        ref[(0,) + index], ref[(1,) + index] = split(values)

    for p in range(2):
        keep(wc, (p, slice(None), slice(0, half)), w_small[2 * p * chan : 2 * (p + 1) * chan])
        first = (p + 1) * 4 * chan + chan
        keep(wc, (p, slice(None), slice(half, feat)), w_large[first : first + 2 * chan])
        first = 3 * p * 4 * chan + chan
        keep(we, (p,), w_large[first : first + 2 * chan])
    for p in range(4):
        keep(wo, (p, slice(0, chan)), w_large[4 * p * chan : (4 * p + 1) * chan])
        keep(wo, (p, slice(chan, 2 * chan)), w_large[(4 * p + 3) * chan : (4 * p + 4) * chan])

    for index in range(8):
        _, arrives, _, _, destination = plan[index]

        @pl.when(arrives)
        def _(index=index):
            halo_copy(index).wait_recv()

        @pl.when(jnp.logical_not(arrives))
        def _(destination=destination):
            destination[...] = jnp.zeros(destination.shape, F32)

    for side, row in ((0, 7), (1, 0)):
        col_halo[side, 7] = corner_halo[side, row]
        col_halo[side, 8 + rows] = corner_halo[2 + side, row]

    first_row = lax.broadcasted_iota(jnp.int32, (tile_cols, 1), 0) == 0
    last_row = lax.broadcasted_iota(jnp.int32, (tile_cols, 1), 0) == tile_cols - 1

    def build(t, source):
        even = source[pl.ds(0, tile_cols, stride=2), :]
        odd = source[pl.ds(1, tile_cols, stride=2), :]
        before = jnp.where(first_row, col_halo[0, pl.ds(t + 7, 1)], pltpu.roll(odd, 1, 0))
        after = jnp.where(last_row, col_halo[1, pl.ds(t + 7, 1)], pltpu.roll(even, tile_cols - 1, 0))
        b, a = t % 2, t // 2
        for hi, lo, left, right in ((eo_hi, eo_lo, even, odd), (oe_hi, oe_lo, before, after)):
            hi[b, a, :, :chan], lo[b, a, :, :chan] = split(left)
            hi[b, a, :, chan:], lo[b, a, :, chan:] = split(right)

    build(0, row_halo.at[0])
    build(1, lat.at[0])
    build(rows + 1, row_halo.at[1])

    def go(s, member):
        rank = place(member)
        return pltpu.make_async_remote_copy(
            src_ref=emb.at[s, member], dst_ref=recv.at[s, me], send_sem=go_send.at[s, member],
            recv_sem=go_recv.at[s, me], device_id=rank, device_id_type=MESH,
        )

    def arrival(s, member):
        return pltpu.make_async_remote_copy(
            src_ref=emb.at[s, member], dst_ref=recv.at[s, member], send_sem=go_send.at[s, member],
            recv_sem=go_recv.at[s, member], device_id=place(member), device_id_type=MESH,
        )

    def home(s, owner):
        return out.at[pl.ds(pl.multiple_of(s * stage_tokens + owner * share, 8), share)]

    def back(s, member):
        return pltpu.make_async_remote_copy(
            src_ref=done.at[s, member], dst_ref=home(s, me), send_sem=back_send.at[s, member],
            recv_sem=back_recv.at[s, me], device_id=place(member), device_id_type=MESH,
        )

    def back_arrival(s, owner):
        return pltpu.make_async_remote_copy(
            src_ref=done.at[s, owner], dst_ref=home(s, owner), send_sem=back_send.at[s, owner],
            recv_sem=back_recv.at[s, owner], device_id=place(owner), device_id_type=MESH,
        )

    def own(s):
        return pltpu.make_async_copy(done.at[s, me], home(s, me), back_recv.at[s, me])

    def embed(s, carry):
        def line(t, inner):
            build(t, lat.at[t - 1])
            return inner

        first = 2 * stage_rows * s + 2
        lax.fori_loop(first, jnp.minimum(first + 2 * stage_rows, rows + 1), line, 0)

        def taps(hi, lo, p):
            where = (p % 2, pl.ds(stage_rows * s + p // 2, stage_rows))
            return tuple(ref[where].reshape(stage_tokens, 2 * chan) for ref in (hi, lo))

        def pair(ref, index):
            return ref[0, index], ref[1, index]

        wide = dot3(taps(eo_hi, eo_lo, 1), pair(wc, 0)) + dot3(taps(eo_hi, eo_lo, 2), pair(wc, 1))
        thin = dot3(taps(eo_hi, eo_lo, 0), pair(we, 0)) + dot3(taps(eo_hi, eo_lo, 3), pair(we, 1))
        for p in range(4):
            thin = thin + dot3(taps(oe_hi, oe_lo, p), pair(wo, p))
        joined = jnp.concatenate([wide[:, :half], wide[:, half:] + thin], axis=-1)
        emb[s] = layer_norm(joined, gain_embed[...]).reshape(members, share, feat)
        recv[s, me] = emb[s, me]

        def send(step, inner):
            go(s, other(step)).start()
            return inner

        lax.fori_loop(1, members, send, 0)
        return carry

    lax.fori_loop(0, STAGES, embed, 0)

    for ref, source in ((wq, w_qkv), (wp, w_proj), (wu, w_up), (wd, w_down)):
        ref[0], ref[1] = split(source[...])

    spread = (
        lax.broadcasted_iota(jnp.int32, (tokens, members), 0) // groups
        == lax.broadcasted_iota(jnp.int32, (tokens, members), 1)
    ).astype(F32)
    same = lax.rem(lax.broadcasted_iota(jnp.int32, (tokens, tokens), 0), groups) == lax.rem(
        lax.broadcasted_iota(jnp.int32, (tokens, tokens), 1), groups
    )
    exact = functools.partial(
        lax.dot_general, precision=lax.Precision.HIGHEST, preferred_element_type=F32
    )

    def widen(h, carry):
        tall = exact(spread, pos_bias[h], (((1,), (0,)), ((), ())))
        bias[h] = jnp.where(same, exact(tall, spread, (((1,), (1,)), ((), ()))), -1e30)
        return carry

    lax.fori_loop(0, HEADS, widen, 0)

    lane_head = lax.broadcasted_iota(jnp.int32, (1, feat), 1) // head
    scale = 1.0 / (head**0.5)

    def block(s, b):
        where = (s, slice(None), pl.ds(pl.multiple_of(b * groups, 8), groups))
        x = recv[where].reshape(tokens, feat)
        normed = split(layer_norm(x, gain_attn[...]))
        qkv = dot3(normed, (wq[0], wq[1]))
        q = qkv[:, :feat] * scale
        k = split(qkv[:, feat : 2 * feat])
        v = split(qkv[:, 2 * feat :])
        mixed = jnp.zeros((tokens, feat), F32)
        for h in range(HEADS):
            mine = lane_head == h
            scores = dot3(split(jnp.where(mine, q, 0.0)), k, ((1,), (1,))) + bias[h]
            expd = jnp.exp(scores - jnp.max(scores, axis=-1, keepdims=True))
            total = jnp.sum(expd, axis=-1, keepdims=True)
            mixed = mixed + jnp.where(mine, dot3(split(expd), v) / total, 0.0)
        after = x + dot3(split(mixed), (wp[0], wp[1]))
        hidden = gelu(dot3(split(layer_norm(after, gain_mlp[...])), (wu[0], wu[1])))
        result = after + dot3(split(hidden), (wd[0], wd[1]))
        done[where] = result.reshape(members, groups, feat)

    def process(s, carry):
        def await_one(step, inner):
            arrival(s, other(step)).wait_recv()
            return inner

        lax.fori_loop(1, members, await_one, 0)

        def work(b, inner):
            block(s, b)
            return inner

        lax.fori_loop(0, share // groups, work, 0)

        def send(step, inner):
            back(s, other(step)).start()
            return inner

        lax.fori_loop(1, members, send, 0)
        own(s).start()
        return carry

    lax.fori_loop(0, STAGES, process, 0)

    def finish(s, carry):
        def each(step, inner):
            member = other(step)
            go(s, member).wait_send()
            back(s, member).wait_send()
            back_arrival(s, member).wait_recv()
            return inner

        lax.fori_loop(1, members, each, 0)
        own(s).wait()
        return carry

    lax.fori_loop(0, STAGES, finish, 0)
    for index in range(8):
        @pl.when(plan[index][0])
        def _(index=index):
            halo_copy(index).wait_send()


def per_device(
    latent, w_small, w_large, gain_embed, gain_attn, w_qkv, pos_bias, w_proj, gain_mlp, w_up, w_down
):
    row_count = lax.axis_size("rows")
    col_count = lax.axis_size("cols")
    samples, rows, cols, chan = latent.shape
    tile_rows, tile_cols = rows // 2, cols // 2
    feat = gain_embed.shape[0]
    half = feat // 2
    members = pos_bias.shape[1]
    phases = row_count // (members // col_count)
    share = tile_rows * tile_cols // STAGES // members
    tokens = members * max(8, min(share, 256 // members))
    pixels = pltpu.VMEM((2, tile_rows + 1, tile_cols, 2 * chan), BF16)
    exchange = pltpu.VMEM((STAGES, members, share, feat), F32)
    dma = pltpu.SemaphoreType.DMA
    vmem = pl.BlockSpec(memory_space=pltpu.VMEM)
    halves = lambda *shape: pltpu.VMEM((2,) + shape, BF16)
    out = pl.pallas_call(
        functools.partial(block_kernel, (row_count, col_count, members, phases)),
        name="crossformer_block",
        out_shape=jax.ShapeDtypeStruct((tile_rows * tile_cols, feat), F32),
        in_specs=[vmem] * 11,
        out_specs=pl.BlockSpec(memory_space=pl.ANY),
        scratch_shapes=[
            pixels, pixels, pixels, pixels,
            halves(2, 2 * chan, feat),
            halves(2, 2 * chan, half),
            halves(4, 2 * chan, half),
            halves(*w_qkv.shape),
            halves(*w_proj.shape),
            halves(*w_up.shape),
            halves(*w_down.shape),
            pltpu.VMEM((HEADS, tokens, tokens), F32),
            exchange, exchange, exchange,
            pltpu.VMEM((2, cols, chan), F32),
            pltpu.VMEM((2, rows + 16, chan), F32),
            pltpu.VMEM((4, 8, chan), F32),
            pltpu.VMEM((2, rows, chan), F32),
            dma((8,)), dma((8,)),
            dma((STAGES, members)), dma((STAGES, members)),
            dma((STAGES, members)), dma((STAGES, members)),
        ],
        compiler_params=pltpu.CompilerParams(
            collective_id=0, has_side_effects=True, vmem_limit_bytes=67043328
        ),
    )(
        latent[0], w_small, w_large, gain_embed[None], gain_attn[None], w_qkv, pos_bias, w_proj,
        gain_mlp[None], w_up, w_down,
    )
    return out.reshape(samples, tile_rows, tile_cols, feat)


def solution(mesh):
    in_specs = (P(None, "rows", "cols", None),) + (P(),) * 10
    out_specs = P(None, "rows", "cols", None)
    return jax.shard_map(
        per_device, mesh=mesh, in_specs=in_specs, out_specs=out_specs, check_vma=False
    )
```

```python
import functools

import jax
import jax.numpy as jnp
from jax import lax
from jax.experimental import pallas as pl
from jax.experimental.pallas import tpu as pltpu
from jax.sharding import PartitionSpec as P

HEADS = 8
STAGES = 4
MESH = pl.DeviceIdType.MESH
F32 = jnp.float32
BF16 = jnp.bfloat16


def split(values):
    high = values.astype(BF16)
    return high, (values - high.astype(F32)).astype(BF16)


def dot(left, right, dims=((1,), (0,))):
    return lax.dot_general(left, right, (dims, ((), ())), preferred_element_type=F32)


def dot3(left, right, dims=((1,), (0,))):
    left_hi, left_lo = left
    right_hi, right_lo = right
    return (
        dot(left_hi, right_lo, dims) + dot(left_lo, right_hi, dims) + dot(left_hi, right_hi, dims)
    )


def layer_norm(values, gain):
    center = values - jnp.mean(values, axis=-1, keepdims=True)
    spread = jnp.mean(center * center, axis=-1, keepdims=True)
    return center * lax.rsqrt(spread + 1e-05) * gain


def gelu(values):
    return 0.5 * values * (1.0 + lax.erf(values * 0.7071067811865476))


def block_kernel(
    sizes,
    *refs,
):
    inputs, out, loaded = refs[:11], refs[11], refs[12:23]
    lat, w_small, w_large, gain_embed, gain_attn, w_qkv, pos_bias, w_proj, gain_mlp, w_up, w_down = loaded
    (
        eo_hi, eo_lo, oe_hi, oe_lo, wc, we, wo, wq, wp, wu, wd, bias,
        emb, recv, done, row_halo, col_halo, corner_halo, col_edge,
        halo_send, halo_recv, go_send, go_recv, back_send, back_recv, load_sem,
    ) = refs[23:]
    row_count, col_count, members, phases = sizes
    rows, cols, chan = lat.shape
    tile_rows, tile_cols = rows // 2, cols // 2
    feat = gain_embed.shape[1]
    half = feat // 2
    stage_rows = tile_rows // STAGES
    stage_tokens = stage_rows * tile_cols
    share = stage_tokens // members
    groups = max(8, min(share, 256 // members))
    tokens = members * groups
    head = feat // HEADS

    r = lax.axis_index("rows")
    c = lax.axis_index("cols")
    core = lax.rem(r, phases)
    me = (r // phases) * col_count + c

    def place(member):
        return (member // col_count) * phases + core, lax.rem(member, col_count)

    def other(step):
        return lax.rem(me + step, members)

    barrier = pltpu.get_barrier_semaphore()

    def greet(step, carry):
        pl.semaphore_signal(barrier, inc=1, device_id=place(other(step)), device_id_type=MESH)
        return carry

    lax.fori_loop(1, members, greet, 0)
    up, down = r > 0, r < row_count - 1
    west, east = c > 0, c < col_count - 1
    for row_ok, dr in ((up, -1), (down, 1)):
        for col_ok, dc in ((True, 0), (west, -1), (east, 1)):
            ok = row_ok if col_ok is True else jnp.logical_and(row_ok, col_ok)

            @pl.when(ok)
            def _(dr=dr, dc=dc):
                pl.semaphore_signal(barrier, inc=1, device_id=(r + dr, c + dc), device_id_type=MESH)

    def load(index):
        return pltpu.make_async_copy(inputs[index], loaded[index], load_sem.at[index])

    for index in range(11):
        load(index).start()
    load(0).wait()
    col_edge[0] = lat[:, 0, :]
    col_edge[1] = lat[:, cols - 1, :]
    number = lambda flag: jnp.where(flag, 1, 0)
    vertical = number(up) + number(down)
    horizontal = 1 + number(west) + number(east)
    pl.semaphore_wait(barrier, members - 1 + vertical * horizontal)

    both = jnp.logical_and
    plan = [
        (up, down, (r - 1, c), lat.at[0], row_halo.at[1]),
        (down, up, (r + 1, c), lat.at[rows - 1], row_halo.at[0]),
        (west, east, (r, c - 1), col_edge.at[0], col_halo.at[1, pl.ds(8, rows)]),
        (east, west, (r, c + 1), col_edge.at[1], col_halo.at[0, pl.ds(8, rows)]),
        (both(up, west), both(down, east), (r - 1, c - 1), lat.at[0, pl.ds(0, 8)], corner_halo.at[3]),
        (both(up, east), both(down, west), (r - 1, c + 1), lat.at[0, pl.ds(cols - 8, 8)], corner_halo.at[2]),
        (both(down, west), both(up, east), (r + 1, c - 1), lat.at[rows - 1, pl.ds(0, 8)], corner_halo.at[1]),
        (both(down, east), both(up, west), (r + 1, c + 1), lat.at[rows - 1, pl.ds(cols - 8, 8)], corner_halo.at[0]),
    ]

    def halo_copy(index):
        _, _, target, source, destination = plan[index]
        return pltpu.make_async_remote_copy(
            src_ref=source, dst_ref=destination, send_sem=halo_send.at[index],
            recv_sem=halo_recv.at[index], device_id=target, device_id_type=MESH,
        )

    for index in range(8):
        @pl.when(plan[index][0])
        def _(index=index):
            halo_copy(index).start()

    first_row = lax.broadcasted_iota(jnp.int32, (tile_cols, 1), 0) == 0
    last_row = lax.broadcasted_iota(jnp.int32, (tile_cols, 1), 0) == tile_cols - 1

    def lay(hi, lo, t, left, right):
        b, a = t % 2, t // 2
        hi[b, a, :, :chan], lo[b, a, :, :chan] = split(left)
        hi[b, a, :, chan:], lo[b, a, :, chan:] = split(right)

    def columns(source):
        return source[pl.ds(0, tile_cols, stride=2), :], source[pl.ds(1, tile_cols, stride=2), :]

    def build_inner(t, source):
        lay(eo_hi, eo_lo, t, *columns(source))

    def build_outer(t, source):
        even, odd = columns(source)
        before = jnp.where(first_row, col_halo[0, pl.ds(t + 7, 1)], pltpu.roll(odd, 1, 0))
        after = jnp.where(last_row, col_halo[1, pl.ds(t + 7, 1)], pltpu.roll(even, tile_cols - 1, 0))
        lay(oe_hi, oe_lo, t, before, after)

    def inner_line(t, carry):
        build_inner(t, lat.at[t - 1])
        return carry

    def outer_line(t, carry):
        build_outer(t, lat.at[t - 1])
        return carry

    def both_lines(t, carry):
        return outer_line(t, inner_line(t, carry))

    lax.fori_loop(1, 2 * stage_rows + 2, inner_line, 0)
    load(1).wait()
    load(2).wait()
    def keep(ref, index, values):
        ref[(0,) + index], ref[(1,) + index] = split(values)

    for p in range(2):
        keep(wc, (p, slice(None), slice(0, half)), w_small[2 * p * chan : 2 * (p + 1) * chan])
        first = (p + 1) * 4 * chan + chan
        keep(wc, (p, slice(None), slice(half, feat)), w_large[first : first + 2 * chan])
        first = 3 * p * 4 * chan + chan
        keep(we, (p,), w_large[first : first + 2 * chan])
    for p in range(4):
        keep(wo, (p, slice(0, chan)), w_large[4 * p * chan : (4 * p + 1) * chan])
        keep(wo, (p, slice(chan, 2 * chan)), w_large[(4 * p + 3) * chan : (4 * p + 4) * chan])

    for index in range(8):
        _, arrives, _, _, destination = plan[index]

        @pl.when(arrives)
        def _(index=index):
            halo_copy(index).wait_recv()

        @pl.when(jnp.logical_not(arrives))
        def _(destination=destination):
            destination[...] = jnp.zeros(destination.shape, F32)

    for side, row in ((0, 7), (1, 0)):
        col_halo[side, 7] = corner_halo[side, row]
        col_halo[side, 8 + rows] = corner_halo[2 + side, row]

    lax.fori_loop(1, 2 * stage_rows + 2, outer_line, 0)
    for t, side in ((0, 0), (rows + 1, 1)):
        build_inner(t, row_halo.at[side])
        build_outer(t, row_halo.at[side])
    for index in range(3, 11):
        load(index).wait()

    def go(s, member):
        rank = place(member)
        return pltpu.make_async_remote_copy(
            src_ref=emb.at[s, member], dst_ref=recv.at[s, me], send_sem=go_send.at[s, member],
            recv_sem=go_recv.at[s, me], device_id=rank, device_id_type=MESH,
        )

    def arrival(s, member):
        return pltpu.make_async_remote_copy(
            src_ref=emb.at[s, member], dst_ref=recv.at[s, member], send_sem=go_send.at[s, member],
            recv_sem=go_recv.at[s, member], device_id=place(member), device_id_type=MESH,
        )

    def home(s, owner):
        return out.at[pl.ds(pl.multiple_of(s * stage_tokens + owner * share, 8), share)]

    def back(s, member):
        return pltpu.make_async_remote_copy(
            src_ref=done.at[s, member], dst_ref=home(s, me), send_sem=back_send.at[s, member],
            recv_sem=back_recv.at[s, me], device_id=place(member), device_id_type=MESH,
        )

    def back_arrival(s, owner):
        return pltpu.make_async_remote_copy(
            src_ref=done.at[s, owner], dst_ref=home(s, owner), send_sem=back_send.at[s, owner],
            recv_sem=back_recv.at[s, owner], device_id=place(owner), device_id_type=MESH,
        )

    def own(s):
        return pltpu.make_async_copy(done.at[s, me], home(s, me), back_recv.at[s, me])

    def embed(s, carry):
        def taps(hi, lo, p):
            where = (p % 2, pl.ds(stage_rows * s + p // 2, stage_rows))
            return tuple(ref[where].reshape(stage_tokens, 2 * chan) for ref in (hi, lo))

        def pair(ref, index):
            return ref[0, index], ref[1, index]

        wide = dot3(taps(eo_hi, eo_lo, 1), pair(wc, 0)) + dot3(taps(eo_hi, eo_lo, 2), pair(wc, 1))
        thin = dot3(taps(eo_hi, eo_lo, 0), pair(we, 0)) + dot3(taps(eo_hi, eo_lo, 3), pair(we, 1))
        for p in range(4):
            thin = thin + dot3(taps(oe_hi, oe_lo, p), pair(wo, p))
        joined = jnp.concatenate([wide[:, :half], wide[:, half:] + thin], axis=-1)
        emb[s] = layer_norm(joined, gain_embed[...]).reshape(members, share, feat)

        def send(step, inner):
            go(s, other(step)).start()
            return inner

        lax.fori_loop(1, members, send, 0)
        recv[s, me] = emb[s, me]
        following = 2 * stage_rows * (s + 1) + 2
        lax.fori_loop(
            following, jnp.minimum(following + 2 * stage_rows, rows + 1), both_lines, 0
        )
        return carry

    lax.fori_loop(0, STAGES, embed, 0)

    for ref, source in ((wq, w_qkv), (wp, w_proj), (wu, w_up), (wd, w_down)):
        ref[0], ref[1] = split(source[...])

    spread = (
        lax.broadcasted_iota(jnp.int32, (tokens, members), 0) // groups
        == lax.broadcasted_iota(jnp.int32, (tokens, members), 1)
    ).astype(F32)
    same = lax.rem(lax.broadcasted_iota(jnp.int32, (tokens, tokens), 0), groups) == lax.rem(
        lax.broadcasted_iota(jnp.int32, (tokens, tokens), 1), groups
    )
    exact = functools.partial(
        lax.dot_general, precision=lax.Precision.HIGHEST, preferred_element_type=F32
    )

    def widen(h, carry):
        tall = exact(spread, pos_bias[h], (((1,), (0,)), ((), ())))
        bias[h] = jnp.where(same, exact(tall, spread, (((1,), (1,)), ((), ()))), -1e30)
        return carry

    lax.fori_loop(0, HEADS, widen, 0)

    lane_head = lax.broadcasted_iota(jnp.int32, (1, feat), 1) // head
    scale = 1.0 / (head**0.5)

    def block(s, b):
        where = (s, slice(None), pl.ds(pl.multiple_of(b * groups, 8), groups))
        x = recv[where].reshape(tokens, feat)
        normed = split(layer_norm(x, gain_attn[...]))
        qkv = dot3(normed, (wq[0], wq[1]))
        q = qkv[:, :feat] * scale
        k = split(qkv[:, feat : 2 * feat])
        v = split(qkv[:, 2 * feat :])
        mixed = jnp.zeros((tokens, feat), F32)
        for h in range(HEADS):
            mine = lane_head == h
            scores = dot3(split(jnp.where(mine, q, 0.0)), k, ((1,), (1,))) + bias[h]
            expd = jnp.exp(scores - jnp.max(scores, axis=-1, keepdims=True))
            total = jnp.sum(expd, axis=-1, keepdims=True)
            mixed = mixed + jnp.where(mine, dot3(split(expd), v) / total, 0.0)
        after = x + dot3(split(mixed), (wp[0], wp[1]))
        hidden = gelu(dot3(split(layer_norm(after, gain_mlp[...])), (wu[0], wu[1])))
        result = after + dot3(split(hidden), (wd[0], wd[1]))
        done[where] = result.reshape(members, groups, feat)

    def process(s, carry):
        def await_one(step, inner):
            arrival(s, other(step)).wait_recv()
            return inner

        lax.fori_loop(1, members, await_one, 0)

        def work(b, inner):
            block(s, b)
            return inner

        lax.fori_loop(0, share // groups, work, 0)

        def send(step, inner):
            back(s, other(step)).start()
            return inner

        lax.fori_loop(1, members, send, 0)
        own(s).start()
        return carry

    lax.fori_loop(0, STAGES, process, 0)

    def finish(s, carry):
        def each(step, inner):
            member = other(step)
            go(s, member).wait_send()
            back(s, member).wait_send()
            back_arrival(s, member).wait_recv()
            return inner

        lax.fori_loop(1, members, each, 0)
        own(s).wait()
        return carry

    lax.fori_loop(0, STAGES, finish, 0)
    for index in range(8):
        @pl.when(plan[index][0])
        def _(index=index):
            halo_copy(index).wait_send()


def per_device(
    latent, w_small, w_large, gain_embed, gain_attn, w_qkv, pos_bias, w_proj, gain_mlp, w_up, w_down
):
    row_count = lax.axis_size("rows")
    col_count = lax.axis_size("cols")
    samples, rows, cols, chan = latent.shape
    tile_rows, tile_cols = rows // 2, cols // 2
    feat = gain_embed.shape[0]
    half = feat // 2
    members = pos_bias.shape[1]
    phases = row_count // (members // col_count)
    share = tile_rows * tile_cols // STAGES // members
    tokens = members * max(8, min(share, 256 // members))
    pixels = pltpu.VMEM((2, tile_rows + 1, tile_cols, 2 * chan), BF16)
    exchange = pltpu.VMEM((STAGES, members, share, feat), F32)
    dma = pltpu.SemaphoreType.DMA
    inputs = (
        latent[0], w_small, w_large, gain_embed[None], gain_attn[None], w_qkv, pos_bias, w_proj,
        gain_mlp[None], w_up, w_down,
    )
    halves = lambda *shape: pltpu.VMEM((2,) + shape, BF16)
    out = pl.pallas_call(
        functools.partial(block_kernel, (row_count, col_count, members, phases)),
        name="crossformer_block",
        out_shape=jax.ShapeDtypeStruct((tile_rows * tile_cols, feat), F32),
        in_specs=[pl.BlockSpec(memory_space=pltpu.HBM)] * 11,
        out_specs=pl.BlockSpec(memory_space=pl.ANY),
        scratch_shapes=[pltpu.VMEM(array.shape, F32) for array in inputs]
        + [
            pixels, pixels, pixels, pixels,
            halves(2, 2 * chan, feat),
            halves(2, 2 * chan, half),
            halves(4, 2 * chan, half),
            halves(*w_qkv.shape),
            halves(*w_proj.shape),
            halves(*w_up.shape),
            halves(*w_down.shape),
            pltpu.VMEM((HEADS, tokens, tokens), F32),
            exchange, exchange, exchange,
            pltpu.VMEM((2, cols, chan), F32),
            pltpu.VMEM((2, rows + 16, chan), F32),
            pltpu.VMEM((4, 8, chan), F32),
            pltpu.VMEM((2, rows, chan), F32),
            dma((8,)), dma((8,)),
            dma((STAGES, members)), dma((STAGES, members)),
            dma((STAGES, members)), dma((STAGES, members)),
            dma((11,)),
        ],
        compiler_params=pltpu.CompilerParams(
            collective_id=0, has_side_effects=True, vmem_limit_bytes=67043328
        ),
    )(*inputs)
    return out.reshape(samples, tile_rows, tile_cols, feat)


def solution(mesh):
    in_specs = (P(None, "rows", "cols", None),) + (P(),) * 10
    out_specs = P(None, "rows", "cols", None)
    return jax.shard_map(
        per_device, mesh=mesh, in_specs=in_specs, out_specs=out_specs, check_vma=False
    )
```

```python
import functools

import jax
import jax.numpy as jnp
from jax import lax
from jax.experimental import pallas as pl
from jax.experimental.pallas import tpu as pltpu
from jax.sharding import PartitionSpec as P

HEADS = 8
STAGES = 4
MESH = pl.DeviceIdType.MESH
F32 = jnp.float32
BF16 = jnp.bfloat16


def split(values):
    high = values.astype(BF16)
    return high, (values - high.astype(F32)).astype(BF16)


def dot(left, right, dims=((1,), (0,))):
    return lax.dot_general(left, right, (dims, ((), ())), preferred_element_type=F32)


def dot3(left, right, dims=((1,), (0,))):
    left_hi, left_lo = left
    right_hi, right_lo = right
    return (
        dot(left_hi, right_lo, dims) + dot(left_lo, right_hi, dims) + dot(left_hi, right_hi, dims)
    )


def layer_norm(values, gain):
    center = values - jnp.mean(values, axis=-1, keepdims=True)
    spread = jnp.mean(center * center, axis=-1, keepdims=True)
    return center * lax.rsqrt(spread + 1e-05) * gain


def gelu(values):
    return 0.5 * values * (1.0 + lax.erf(values * 0.7071067811865476))


def block_kernel(
    sizes,
    *refs,
):
    inputs, out, loaded = refs[:11], refs[11], refs[12:23]
    lat, w_small, w_large, gain_embed, gain_attn, w_qkv, pos_bias, w_proj, gain_mlp, w_up, w_down = loaded
    (
        eo_hi, eo_lo, oe_hi, oe_lo, wc, we, wo, wq, wp, wu, wd, bias,
        emb, recv, done, row_halo, col_halo, corner_halo, col_edge,
        halo_send, halo_recv, go_send, go_recv, back_send, back_recv, load_sem,
    ) = refs[23:]
    row_count, col_count, members, phases = sizes
    rows, cols, chan = lat.shape
    tile_rows, tile_cols = rows // 2, cols // 2
    feat = gain_embed.shape[1]
    half = feat // 2
    stage_rows = tile_rows // STAGES
    stage_tokens = stage_rows * tile_cols
    share = stage_tokens // members
    groups = max(8, min(share, 256 // members))
    tokens = members * groups
    head = feat // HEADS

    r = lax.axis_index("rows")
    c = lax.axis_index("cols")
    core = lax.rem(r, phases)
    me = (r // phases) * col_count + c

    def place(member):
        return (member // col_count) * phases + core, lax.rem(member, col_count)

    def other(step):
        per = members // col_count
        g = (step - 1) // per
        dk = lax.rem(step, per)
        dc = lax.rem(col_count // 2 + (g + 1) // 2 * (2 * lax.rem(g, 2) - 1) + col_count, col_count)
        return lax.rem(me // col_count + dk, per) * col_count + lax.rem(c + dc, col_count)

    barrier = pltpu.get_barrier_semaphore()

    def greet(step, carry):
        pl.semaphore_signal(barrier, inc=1, device_id=place(other(step)), device_id_type=MESH)
        return carry

    lax.fori_loop(1, members, greet, 0)
    up, down = r > 0, r < row_count - 1
    west, east = c > 0, c < col_count - 1
    for row_ok, dr in ((up, -1), (down, 1)):
        for col_ok, dc in ((True, 0), (west, -1), (east, 1)):
            ok = row_ok if col_ok is True else jnp.logical_and(row_ok, col_ok)

            @pl.when(ok)
            def _(dr=dr, dc=dc):
                pl.semaphore_signal(barrier, inc=1, device_id=(r + dr, c + dc), device_id_type=MESH)

    def load(index):
        return pltpu.make_async_copy(inputs[index], loaded[index], load_sem.at[index])

    for index in range(11):
        load(index).start()
    load(0).wait()
    col_edge[0] = lat[:, 0, :]
    col_edge[1] = lat[:, cols - 1, :]
    number = lambda flag: jnp.where(flag, 1, 0)
    vertical = number(up) + number(down)
    horizontal = 1 + number(west) + number(east)
    pl.semaphore_wait(barrier, members - 1 + vertical * horizontal)

    both = jnp.logical_and
    plan = [
        (up, down, (r - 1, c), lat.at[0], row_halo.at[1]),
        (down, up, (r + 1, c), lat.at[rows - 1], row_halo.at[0]),
        (west, east, (r, c - 1), col_edge.at[0], col_halo.at[1, pl.ds(8, rows)]),
        (east, west, (r, c + 1), col_edge.at[1], col_halo.at[0, pl.ds(8, rows)]),
        (both(up, west), both(down, east), (r - 1, c - 1), lat.at[0, pl.ds(0, 8)], corner_halo.at[3]),
        (both(up, east), both(down, west), (r - 1, c + 1), lat.at[0, pl.ds(cols - 8, 8)], corner_halo.at[2]),
        (both(down, west), both(up, east), (r + 1, c - 1), lat.at[rows - 1, pl.ds(0, 8)], corner_halo.at[1]),
        (both(down, east), both(up, west), (r + 1, c + 1), lat.at[rows - 1, pl.ds(cols - 8, 8)], corner_halo.at[0]),
    ]

    def halo_copy(index):
        _, _, target, source, destination = plan[index]
        return pltpu.make_async_remote_copy(
            src_ref=source, dst_ref=destination, send_sem=halo_send.at[index],
            recv_sem=halo_recv.at[index], device_id=target, device_id_type=MESH,
        )

    for index in range(8):
        @pl.when(plan[index][0])
        def _(index=index):
            halo_copy(index).start()

    first_row = lax.broadcasted_iota(jnp.int32, (tile_cols, 1), 0) == 0
    last_row = lax.broadcasted_iota(jnp.int32, (tile_cols, 1), 0) == tile_cols - 1

    def lay(hi, lo, t, left, right):
        b, a = t % 2, t // 2
        hi[b, a, :, :chan], lo[b, a, :, :chan] = split(left)
        hi[b, a, :, chan:], lo[b, a, :, chan:] = split(right)

    def columns(source):
        return source[pl.ds(0, tile_cols, stride=2), :], source[pl.ds(1, tile_cols, stride=2), :]

    def build_inner(t, source):
        lay(eo_hi, eo_lo, t, *columns(source))

    def build_outer(t, source):
        even, odd = columns(source)
        before = jnp.where(first_row, col_halo[0, pl.ds(t + 7, 1)], pltpu.roll(odd, 1, 0))
        after = jnp.where(last_row, col_halo[1, pl.ds(t + 7, 1)], pltpu.roll(even, tile_cols - 1, 0))
        lay(oe_hi, oe_lo, t, before, after)

    def inner_line(t, carry):
        build_inner(t, lat.at[t - 1])
        return carry

    def outer_line(t, carry):
        build_outer(t, lat.at[t - 1])
        return carry

    def both_lines(t, carry):
        return outer_line(t, inner_line(t, carry))

    lax.fori_loop(1, 2 * stage_rows + 2, inner_line, 0)
    load(1).wait()
    load(2).wait()
    def keep(ref, index, values):
        ref[(0,) + index], ref[(1,) + index] = split(values)

    for p in range(2):
        keep(wc, (p, slice(None), slice(0, half)), w_small[2 * p * chan : 2 * (p + 1) * chan])
        first = (p + 1) * 4 * chan + chan
        keep(wc, (p, slice(None), slice(half, feat)), w_large[first : first + 2 * chan])
        first = 3 * p * 4 * chan + chan
        keep(we, (p,), w_large[first : first + 2 * chan])
    for p in range(4):
        keep(wo, (p, slice(0, chan)), w_large[4 * p * chan : (4 * p + 1) * chan])
        keep(wo, (p, slice(chan, 2 * chan)), w_large[(4 * p + 3) * chan : (4 * p + 4) * chan])

    for index in range(8):
        _, arrives, _, _, destination = plan[index]

        @pl.when(arrives)
        def _(index=index):
            halo_copy(index).wait_recv()

        @pl.when(jnp.logical_not(arrives))
        def _(destination=destination):
            destination[...] = jnp.zeros(destination.shape, F32)

    for side, row in ((0, 7), (1, 0)):
        col_halo[side, 7] = corner_halo[side, row]
        col_halo[side, 8 + rows] = corner_halo[2 + side, row]

    lax.fori_loop(1, 2 * stage_rows + 2, outer_line, 0)
    for t, side in ((0, 0), (rows + 1, 1)):
        build_inner(t, row_halo.at[side])
        build_outer(t, row_halo.at[side])
    for index in range(3, 11):
        load(index).wait()

    def go(s, member):
        rank = place(member)
        return pltpu.make_async_remote_copy(
            src_ref=emb.at[s, member], dst_ref=recv.at[s, me], send_sem=go_send.at[s, member],
            recv_sem=go_recv.at[s, me], device_id=rank, device_id_type=MESH,
        )

    def arrival(s, member):
        return pltpu.make_async_remote_copy(
            src_ref=emb.at[s, member], dst_ref=recv.at[s, member], send_sem=go_send.at[s, member],
            recv_sem=go_recv.at[s, member], device_id=place(member), device_id_type=MESH,
        )

    def home(s, owner):
        return out.at[pl.ds(pl.multiple_of(s * stage_tokens + owner * share, 8), share)]

    def back(s, member):
        return pltpu.make_async_remote_copy(
            src_ref=done.at[s, member], dst_ref=home(s, me), send_sem=back_send.at[s, member],
            recv_sem=back_recv.at[s, me], device_id=place(member), device_id_type=MESH,
        )

    def back_arrival(s, owner):
        return pltpu.make_async_remote_copy(
            src_ref=done.at[s, owner], dst_ref=home(s, owner), send_sem=back_send.at[s, owner],
            recv_sem=back_recv.at[s, owner], device_id=place(owner), device_id_type=MESH,
        )

    def own(s):
        return pltpu.make_async_copy(done.at[s, me], home(s, me), back_recv.at[s, me])

    def embed(s, carry):
        def taps(hi, lo, p):
            where = (p % 2, pl.ds(stage_rows * s + p // 2, stage_rows))
            return tuple(ref[where].reshape(stage_tokens, 2 * chan) for ref in (hi, lo))

        def pair(ref, index):
            return ref[0, index], ref[1, index]

        wide = dot3(taps(eo_hi, eo_lo, 1), pair(wc, 0)) + dot3(taps(eo_hi, eo_lo, 2), pair(wc, 1))
        thin = dot3(taps(eo_hi, eo_lo, 0), pair(we, 0)) + dot3(taps(eo_hi, eo_lo, 3), pair(we, 1))
        for p in range(4):
            thin = thin + dot3(taps(oe_hi, oe_lo, p), pair(wo, p))
        joined = jnp.concatenate([wide[:, :half], wide[:, half:] + thin], axis=-1)
        emb[s] = layer_norm(joined, gain_embed[...]).reshape(members, share, feat)

        def send(step, inner):
            go(s, other(step)).start()
            return inner

        lax.fori_loop(1, members, send, 0)
        recv[s, me] = emb[s, me]
        following = 2 * stage_rows * (s + 1) + 2
        lax.fori_loop(
            following, jnp.minimum(following + 2 * stage_rows, rows + 1), both_lines, 0
        )
        return carry

    lax.fori_loop(0, STAGES, embed, 0)

    for ref, source in ((wq, w_qkv), (wp, w_proj), (wu, w_up), (wd, w_down)):
        ref[0], ref[1] = split(source[...])

    spread = (
        lax.broadcasted_iota(jnp.int32, (tokens, members), 0) // groups
        == lax.broadcasted_iota(jnp.int32, (tokens, members), 1)
    ).astype(F32)
    same = lax.rem(lax.broadcasted_iota(jnp.int32, (tokens, tokens), 0), groups) == lax.rem(
        lax.broadcasted_iota(jnp.int32, (tokens, tokens), 1), groups
    )
    exact = functools.partial(
        lax.dot_general, precision=lax.Precision.HIGHEST, preferred_element_type=F32
    )

    def widen(h, carry):
        tall = exact(spread, pos_bias[h], (((1,), (0,)), ((), ())))
        bias[h] = jnp.where(same, exact(tall, spread, (((1,), (1,)), ((), ()))), -1e30)
        return carry

    lax.fori_loop(0, HEADS, widen, 0)

    lane_head = lax.broadcasted_iota(jnp.int32, (1, feat), 1) // head
    scale = 1.0 / (head**0.5)

    def block(s, b):
        where = (s, slice(None), pl.ds(pl.multiple_of(b * groups, 8), groups))
        x = recv[where].reshape(tokens, feat)
        normed = split(layer_norm(x, gain_attn[...]))
        qkv = dot3(normed, (wq[0], wq[1]))
        q = qkv[:, :feat] * scale
        k = split(qkv[:, feat : 2 * feat])
        v = split(qkv[:, 2 * feat :])
        mixed = jnp.zeros((tokens, feat), F32)
        for h in range(HEADS):
            mine = lane_head == h
            scores = dot3(split(jnp.where(mine, q, 0.0)), k, ((1,), (1,))) + bias[h]
            expd = jnp.exp(scores - jnp.max(scores, axis=-1, keepdims=True))
            total = jnp.sum(expd, axis=-1, keepdims=True)
            mixed = mixed + jnp.where(mine, dot3(split(expd), v) / total, 0.0)
        after = x + dot3(split(mixed), (wp[0], wp[1]))
        hidden = gelu(dot3(split(layer_norm(after, gain_mlp[...])), (wu[0], wu[1])))
        result = after + dot3(split(hidden), (wd[0], wd[1]))
        done[where] = result.reshape(members, groups, feat)

    def process(s, carry):
        def await_one(step, inner):
            arrival(s, other(step)).wait_recv()
            return inner

        lax.fori_loop(1, members, await_one, 0)

        def work(b, inner):
            block(s, b)
            return inner

        lax.fori_loop(0, share // groups, work, 0)

        def send(step, inner):
            back(s, other(step)).start()
            return inner

        lax.fori_loop(1, members, send, 0)
        own(s).start()
        return carry

    lax.fori_loop(0, STAGES, process, 0)

    def finish(s, carry):
        def each(step, inner):
            member = other(step)
            go(s, member).wait_send()
            back(s, member).wait_send()
            back_arrival(s, member).wait_recv()
            return inner

        lax.fori_loop(1, members, each, 0)
        own(s).wait()
        return carry

    lax.fori_loop(0, STAGES, finish, 0)
    for index in range(8):
        @pl.when(plan[index][0])
        def _(index=index):
            halo_copy(index).wait_send()


def per_device(
    latent, w_small, w_large, gain_embed, gain_attn, w_qkv, pos_bias, w_proj, gain_mlp, w_up, w_down
):
    row_count = lax.axis_size("rows")
    col_count = lax.axis_size("cols")
    samples, rows, cols, chan = latent.shape
    tile_rows, tile_cols = rows // 2, cols // 2
    feat = gain_embed.shape[0]
    half = feat // 2
    members = pos_bias.shape[1]
    phases = row_count // (members // col_count)
    share = tile_rows * tile_cols // STAGES // members
    tokens = members * max(8, min(share, 256 // members))
    pixels = pltpu.VMEM((2, tile_rows + 1, tile_cols, 2 * chan), BF16)
    exchange = pltpu.VMEM((STAGES, members, share, feat), F32)
    dma = pltpu.SemaphoreType.DMA
    inputs = (
        latent[0], w_small, w_large, gain_embed[None], gain_attn[None], w_qkv, pos_bias, w_proj,
        gain_mlp[None], w_up, w_down,
    )
    halves = lambda *shape: pltpu.VMEM((2,) + shape, BF16)
    out = pl.pallas_call(
        functools.partial(block_kernel, (row_count, col_count, members, phases)),
        name="crossformer_block",
        out_shape=jax.ShapeDtypeStruct((tile_rows * tile_cols, feat), F32),
        in_specs=[pl.BlockSpec(memory_space=pltpu.HBM)] * 11,
        out_specs=pl.BlockSpec(memory_space=pl.ANY),
        scratch_shapes=[pltpu.VMEM(array.shape, F32) for array in inputs]
        + [
            pixels, pixels, pixels, pixels,
            halves(2, 2 * chan, feat),
            halves(2, 2 * chan, half),
            halves(4, 2 * chan, half),
            halves(*w_qkv.shape),
            halves(*w_proj.shape),
            halves(*w_up.shape),
            halves(*w_down.shape),
            pltpu.VMEM((HEADS, tokens, tokens), F32),
            exchange, exchange, exchange,
            pltpu.VMEM((2, cols, chan), F32),
            pltpu.VMEM((2, rows + 16, chan), F32),
            pltpu.VMEM((4, 8, chan), F32),
            pltpu.VMEM((2, rows, chan), F32),
            dma((8,)), dma((8,)),
            dma((STAGES, members)), dma((STAGES, members)),
            dma((STAGES, members)), dma((STAGES, members)),
            dma((11,)),
        ],
        compiler_params=pltpu.CompilerParams(
            collective_id=0, has_side_effects=True, vmem_limit_bytes=67043328
        ),
    )(*inputs)
    return out.reshape(samples, tile_rows, tile_cols, feat)


def solution(mesh):
    in_specs = (P(None, "rows", "cols", None),) + (P(),) * 10
    out_specs = P(None, "rows", "cols", None)
    return jax.shard_map(
        per_device, mesh=mesh, in_specs=in_specs, out_specs=out_specs, check_vma=False
    )
```
